512 devices in a mesh: dp: 64 (over x, z), ctx: 8 (over y, core).
Axes of the slice: x: 4, y: 4, z: 16, core: 2. Of those that a mesh axis runs over, the one named last changes fastest.
Arguments:
- projections: bfloat16 [131072, 6144], P(('dp', 'ctx')), may hold values from -6 to 6
- block_source: int32 [64, 8, 2], P('dp', 'ctx'), may hold values from 0 to 1023, as said below
- clip_ids: int32 [64, 16], P('dp'), may hold values from 0 to 8, as said below
- out_weight: bfloat16 [2048, 1536], P('dp'), may hold values from -1 to 1
Outputs:
- mixed: bfloat16 [131072, 1536], P(('dp', 'ctx'))
The draws below stay inside these ranges and needn't reach their ends.
Inputs may be any that keep to these rules, and one draw needn't show every extreme that they name: `block_source`: arrival block a lies on the device numbered a // 2 in dp-major order (dp index a // (2 * 8), ctx index (a // 2) % 8). The block that fills pack block (o, j, l) lies on the device with the same ctx index j and dp index o or o XOR 1. Every arrival block fills exactly one pack block. `clip_ids`: in each pack the clip numbers start at 0, never fall and rise by at most one from block to block; every clip spans 1 to 8 blocks, and in every pack some clip spans exactly 8 blocks.
All inputs are finite; a program needn't handle non-finite values.
Results may differ from the reference program's by a relative error of at most 0.0057.
Values may be sent and summed in bfloat16 or wider, within the bound.
A program may use at most 64 MiB of HBM per device.

```python
import math
import jax
import jax.numpy as jnp
from jax import lax

HEADS = 16
HEAD = 128
DOUT = 1536
BLK = 128
BLK_DEV = 2
HW = 2048
ROWS = 131072
N_DP = 64
N_CTX = 8


def draw_projections(key, part):
    key_base = jax.random.fold_in(key, 0)
    drawn = jnp.clip(jax.random.normal(key_base, (ROWS, HEADS, 3, HEAD), jnp.float32), -6.0, 6.0)
    return drawn.reshape(ROWS, HEADS * 3 * HEAD).astype(jnp.bfloat16)


def draw_block_source(key, part):
    window_size = 2 * BLK_DEV
    pair_count = N_DP // 2
    key_scores, key_force = jax.random.split(jax.random.fold_in(key, 11))
    scores = jax.random.randint(key_scores, (N_CTX, pair_count, window_size), 0, 1 << 20)
    scores = scores * window_size + jnp.arange(window_size, dtype=jnp.int32)
    shuffled = jnp.argsort(scores, axis=-1).astype(jnp.int32)
    forced = jax.random.randint(key_force, (N_CTX,), 0, pair_count)
    swapped = (jnp.arange(window_size, dtype=jnp.int32) + BLK_DEV) % window_size
    is_forced = jnp.arange(pair_count, dtype=jnp.int32)[None, :] == forced[:, None]
    shuffled = jnp.where(is_forced[:, :, None], swapped[None, None, :], shuffled)
    source_dp = 2 * jnp.arange(pair_count, dtype=jnp.int32)[None, :, None] + shuffled // BLK_DEV
    source_slot = shuffled % BLK_DEV
    column = jnp.arange(N_CTX, dtype=jnp.int32)[:, None, None]
    arrival = (source_dp * N_CTX + column) * BLK_DEV + source_slot
    arranged = arrival.reshape(N_CTX, N_DP, BLK_DEV)
    return jnp.transpose(arranged, (1, 0, 2)).astype(jnp.int32)


def draw_clip_ids(key, part):
    pack_blocks = BLK_DEV * N_CTX
    longest = max(pack_blocks // 2, 1)
    key_length, key_which, key_pack = jax.random.split(jax.random.fold_in(key, 23), 3)
    lengths = jax.random.randint(key_length, (N_DP, pack_blocks), 1, longest + 1)
    chosen_pack = jax.random.randint(key_pack, (), 0, N_DP)
    pack_order = jnp.arange(N_DP, dtype=jnp.int32)
    lengths = jnp.where((pack_order == chosen_pack)[:, None], 1, lengths)
    which = jax.random.randint(key_which, (N_DP,), 0, 2)
    positions = jnp.arange(pack_blocks, dtype=jnp.int32)
    lengths = jnp.where(positions[None, :] == which[:, None], longest, lengths)
    ends = jnp.cumsum(lengths, axis=1)
    clip_number = jnp.sum((ends[:, None, :] <= positions[None, :, None]).astype(jnp.int32), axis=2)
    return clip_number.astype(jnp.int32)


def steps_of(stream_key, dims, cuts, smallest, top_value):
    loudness = 1.0
    for position, blocks in cuts:
        draws = jax.random.uniform(jax.random.fold_in(jax.random.fold_in(stream_key, 6), position), (blocks,), jnp.float32, smallest / len(cuts), top_value / len(cuts))
        loudness = loudness * jnp.repeat(jnp.exp(draws), dims[position] // blocks).reshape((-1,) + (1,) * (len(dims) - 1 - position))
    return loudness


def noise(key, extent, scale, reach, cuts=(), held_as=jnp.bfloat16):
    array = scale * jax.random.normal(key, extent, jnp.float32)
    if cuts:
        array = array * steps_of(key, extent, cuts, -0.22, 0.18)
    return jnp.clip(array, -reach, reach).astype(held_as)


def setup_inputs(seed: int = 0) -> dict:
    key_of = jax.random.split(jax.random.key(seed), 5)
    return {
        "projections": draw_projections(jax.random.fold_in(key_of[4], 71), 0),
        "block_source": draw_block_source(jax.random.fold_in(key_of[4], 71), 0),
        "clip_ids": draw_clip_ids(jax.random.fold_in(key_of[4], 71), 0),
        "out_weight": noise(key_of[3], (HW, DOUT), (HW // 64) ** -0.5, 1.0, ((0, 64),)),
    }


big_negative = -1e+30

def soft_weights(scores, allowed):
    masked = jnp.where(allowed, scores, big_negative)
    row_max = lax.optimization_barrier(jnp.max(masked, axis=-1, keepdims=True))
    exponent = jnp.exp(masked - row_max)
    return (exponent / lax.optimization_barrier(jnp.sum(exponent, axis=-1, keepdims=True))).astype(jnp.bfloat16)

def reference(projections, block_source, clip_ids, out_weight):
    pack_rows = BLK_DEV * N_CTX * BLK
    blocks = projections.reshape(-1, BLK, HEADS * 3 * HEAD)
    packed = jnp.take(blocks, block_source.reshape(-1).astype(jnp.int32), axis=0)
    packed = packed.reshape(N_DP, pack_rows, HEADS, 3, HEAD)
    scaling = 1.0 / math.sqrt(HEAD)

    def one_pack(arguments):
        pack, clips = arguments
        token_clip = jnp.repeat(clips, BLK)
        allowed = token_clip[:, None] == token_clip[None, :]
        by_head = jnp.transpose(pack, (1, 0, 2, 3))

        def one_head(head_data):
            queries = head_data[:, 0].astype(jnp.float32)
            key_rows = head_data[:, 1].astype(jnp.float32)
            value_rows = head_data[:, 2].astype(jnp.float32)
            scores = jnp.einsum('qe,ke->qk', queries, key_rows) * scaling
            weights = soft_weights(scores, allowed)
            return jnp.einsum('qk,ke->qe', weights.astype(jnp.float32), value_rows).astype(jnp.bfloat16)
        attended = lax.map(one_head, by_head)
        attended = jnp.transpose(attended, (1, 0, 2)).reshape(pack_rows, HEADS * HEAD)
        return jnp.dot(attended, out_weight, preferred_element_type=jnp.float32).astype(jnp.bfloat16)
    outputs = lax.map(one_pack, (packed, clip_ids))
    return outputs.reshape(N_DP * pack_rows, DOUT)
```

```python
import functools
import math

import jax
import jax.numpy as jnp
from jax import lax
from jax.experimental import pallas as pl
from jax.experimental.pallas import tpu as pltpu
from jax.sharding import PartitionSpec as P

HEAD = 128
BLK = 128
PACK = 16
WIN = 8
GROUP = 16
MESH = pl.DeviceIdType.MESH
NEG = -1e30
EXP2_SCALE = math.log2(math.e) / math.sqrt(HEAD)
PEERS = [
    (1, 0, 0), (0, 1, 0), (0, 3, 0), (1, 1, 0), (0, 2, 0), (1, 3, 0), (0, 1, 1), (1, 2, 0),
    (0, 3, 1), (1, 0, 1), (0, 2, 1), (1, 1, 1), (1, 3, 1), (1, 2, 1), (0, 0, 1),
]


def place(ds, dy, dc):
    dp = lax.axis_index("dp")
    ctx = lax.axis_index("ctx")
    side = dp % 2
    to_side = (side + ds) % 2
    to_ctx = ((ctx // 2 + dy) % 4) * 2 + (ctx % 2 + dc) % 2
    return (dp - side + to_side, to_ctx), to_side * 8 + to_ctx


def kernel(
    meta_ref, proj_ref, out_ref,
    q_recv, k_recv, v_recv, meta_recv, meta_smem, k_pack, v_pack, probs, sent, merged,
    send_sem, recv_sem, meta_send, meta_sem, out_send, out_sem, local_sem,
):
    recv = (q_recv, k_recv, v_recv)
    me = (lax.axis_index("dp") % 2) * 8 + lax.axis_index("ctx")

    def columns(rank, kind):
        return pl.ds(pl.multiple_of(rank * (3 * HEAD) + kind * HEAD, HEAD), HEAD)

    own = []
    for kind in range(3):
        own.append(
            pltpu.make_async_copy(
                proj_ref.at[:, :, columns(me, kind)], recv[kind].at[pl.ds(2 * me, 2)], local_sem.at[kind]
            )
        )
    own.append(pltpu.make_async_copy(meta_ref, meta_recv.at[me], local_sem.at[3]))
    for copy in own:
        copy.start()

    barrier = pltpu.get_barrier_semaphore()
    for peer in PEERS:
        device, _ = place(*peer)
        pl.semaphore_signal(barrier, inc=1, device_id=device, device_id_type=MESH)
    pl.semaphore_wait(barrier, len(PEERS))

    started = []
    for i, peer in enumerate(PEERS):
        device, rank = place(*peer)
        started.append(
            pltpu.make_async_remote_copy(
                src_ref=meta_ref, dst_ref=meta_recv.at[me], send_sem=meta_send.at[i],
                recv_sem=meta_sem.at[me], device_id=device, device_id_type=MESH,
            )
        )
        started[-1].start()
    for kind in (1, 0, 2):
        for i, peer in enumerate(PEERS):
            device, rank = place(*peer)
            started.append(
                pltpu.make_async_remote_copy(
                    src_ref=proj_ref.at[:, :, columns(rank, kind)], dst_ref=recv[kind].at[pl.ds(2 * me, 2)],
                    send_sem=send_sem.at[kind, i], recv_sem=recv_sem.at[kind, me],
                    device_id=device, device_id_type=MESH,
                )
            )
            started[-1].start()

    def wait_kind(kind):
        for i, peer in enumerate(PEERS):
            device, rank = place(*peer)
            pltpu.make_async_remote_copy(
                src_ref=recv[kind].at[pl.ds(2 * rank, 2)], dst_ref=recv[kind].at[pl.ds(2 * rank, 2)],
                send_sem=send_sem.at[kind, i], recv_sem=recv_sem.at[kind, rank],
                device_id=device, device_id_type=MESH,
            ).wait_recv()
        own[kind].wait()

    for i, peer in enumerate(PEERS):
        device, rank = place(*peer)
        pltpu.make_async_remote_copy(
            src_ref=meta_recv.at[rank], dst_ref=meta_recv.at[rank], send_sem=meta_send.at[i],
            recv_sem=meta_sem.at[rank], device_id=device, device_id_type=MESH,
        ).wait_recv()
    own[3].wait()
    to_smem = pltpu.make_async_copy(meta_recv, meta_smem, local_sem.at[4])
    to_smem.start()
    to_smem.wait()

    def source(pack, block):
        return meta_smem[pack * 8 + block // 2, 0, block % 2]

    def clip(pack, block):
        return meta_smem[pack * 8, 0, 2 + block]

    def window(pack, block):
        first = block
        for back in range(1, WIN):
            at = jnp.maximum(block - back, 0)
            first = jnp.where(clip(pack, at) == clip(pack, block), jnp.minimum(first, at), first)
        return jnp.minimum(first, PACK - WIN)

    def gather(kind, target):
        def step(i, carry):
            target[i, :, pl.ds(0, HEAD)] = recv[kind][source(i // PACK, i % PACK)]
            return carry

        lax.fori_loop(0, 2 * PACK, step, 0)

    v_pack[:, :, HEAD:] = jnp.ones((2 * PACK, BLK, HEAD), jnp.bfloat16)
    wait_kind(1)
    gather(1, k_pack)
    wait_kind(0)

    def score_step(i, carry):
        pack, block = i // PACK, i % PACK
        start = window(pack, block)
        queries = q_recv[source(pack, block)]
        keys = k_pack[pl.ds(pack * PACK + start, WIN)].reshape(WIN * BLK, HEAD)
        scores = lax.dot_general(queries, keys, (((1,), (1,)), ((), ())), preferred_element_type=jnp.float32)
        parts = []
        for w in range(WIN):
            bias = jnp.where(clip(pack, start + w) == clip(pack, block), 0.0, NEG)
            parts.append(scores[:, w * BLK : (w + 1) * BLK] + bias)
        top = functools.reduce(jnp.maximum, parts)
        row_max = jnp.max(top, axis=1, keepdims=True)
        for w in range(WIN):
            probs[i, :, w * BLK : (w + 1) * BLK] = jnp.exp2((parts[w] - row_max) * EXP2_SCALE).astype(jnp.bfloat16)
        return carry

    lax.fori_loop(0, 2 * PACK, score_step, 0)
    wait_kind(2)
    gather(2, v_pack)

    def attend(rank):
        pack = rank // 8
        for slot in range(2):
            block = (rank % 8) * 2 + slot
            i = pack * PACK + block
            values = v_pack[pl.ds(pack * PACK + window(pack, block), WIN)].reshape(WIN * BLK, 2 * HEAD)
            total = jnp.dot(probs[i], values, preferred_element_type=jnp.float32)
            sent[rank, slot] = (total[:, :HEAD] / total[:, HEAD:]).astype(jnp.bfloat16)

    def my_columns(rank):
        return pl.ds(pl.multiple_of(rank * HEAD, HEAD), HEAD)

    def send_step(k, carry):
        ds, dy, dc = k % 2, (k // 2) % 4, k // 8
        device, rank = place(ds, dy, dc)
        attend(rank)
        pltpu.make_async_remote_copy(
            src_ref=sent.at[rank], dst_ref=merged.at[:, :, my_columns(me)], send_sem=out_send.at[k],
            recv_sem=out_sem.at[me], device_id=device, device_id_type=MESH,
        ).start()
        return carry

    lax.fori_loop(1, GROUP, send_step, 0)
    attend(me)
    keep = pltpu.make_async_copy(sent.at[me], merged.at[:, :, my_columns(me)], local_sem.at[3])
    keep.start()
    keep.wait()
    for k in range(1, GROUP):
        device, rank = place(k % 2, (k // 2) % 4, k // 8)
        copy = pltpu.make_async_remote_copy(
            src_ref=sent.at[rank], dst_ref=merged.at[:, :, my_columns(rank)], send_sem=out_send.at[k],
            recv_sem=out_sem.at[rank], device_id=device, device_id_type=MESH,
        )
        copy.wait_send()
        copy.wait_recv()
    for copy in started:
        copy.wait_send()
    finish = pltpu.make_async_copy(merged, out_ref, local_sem.at[4])
    finish.start()
    finish.wait()


def body(projections, block_source, clip_ids, out_weight):
    rows, width = projections.shape
    heads = width // (3 * HEAD)
    meta = jnp.concatenate([block_source.reshape(-1) % (2 * PACK), clip_ids.reshape(-1)])
    meta = jnp.pad(meta[None, :], ((0, 7), (0, 128 - meta.shape[0])))
    kinds = pltpu.SemaphoreType.DMA((3, GROUP))
    ranks = pltpu.SemaphoreType.DMA((GROUP,))
    attended = pl.pallas_call(
        kernel,
        out_shape=jax.ShapeDtypeStruct((2, BLK, heads * HEAD), jnp.bfloat16),
        in_specs=[pl.BlockSpec(memory_space=pl.ANY)] * 2,
        out_specs=pl.BlockSpec(memory_space=pl.ANY),
        scratch_shapes=[
            pltpu.VMEM((2 * PACK, BLK, HEAD), jnp.bfloat16),
            pltpu.VMEM((2 * PACK, BLK, HEAD), jnp.bfloat16),
            pltpu.VMEM((2 * PACK, BLK, HEAD), jnp.bfloat16),
            pltpu.VMEM((GROUP, 8, 128), jnp.int32),
            pltpu.SMEM((GROUP, 8, 128), jnp.int32),
            pltpu.VMEM((2 * PACK, BLK, HEAD), jnp.bfloat16),
            pltpu.VMEM((2 * PACK, BLK, 2 * HEAD), jnp.bfloat16),
            pltpu.VMEM((2 * PACK, BLK, WIN * BLK), jnp.bfloat16),
            pltpu.VMEM((GROUP, 2, BLK, HEAD), jnp.bfloat16),
            pltpu.VMEM((2, BLK, heads * HEAD), jnp.bfloat16),
            kinds, kinds, ranks, ranks, ranks, ranks,
            pltpu.SemaphoreType.DMA((5,)),
        ],
        compiler_params=pltpu.CompilerParams(
            collective_id=0, has_side_effects=True, vmem_limit_bytes=48 * 2**20
        ),
        name="attend",
    )(meta, projections.reshape(2, BLK, width))
    result = jnp.dot(
        attended.reshape(rows, heads * HEAD),
        lax.all_gather(out_weight, "dp", axis=0, tiled=True),
        preferred_element_type=jnp.float32,
    )
    return result.astype(jnp.bfloat16)


def solution(mesh):
    return jax.shard_map(
        body,
        mesh=mesh,
        in_specs=(P(("dp", "ctx"), None), P("dp", "ctx", None), P("dp", None), P("dp", None)),
        out_specs=P(("dp", "ctx"), None),
        check_vma=False,
    )
```

```python
import functools
import math

import jax
import jax.numpy as jnp
from jax import lax
from jax.experimental import pallas as pl
from jax.experimental.pallas import tpu as pltpu
from jax.sharding import PartitionSpec as P

HEAD = 128
BLK = 128
PACK = 16
WIN = 8
GROUP = 16
MESH = pl.DeviceIdType.MESH
N_X, N_Z = 4, 16
TILE = 256
FIRST, BATCH, EARLY = 10, 7, 5
NEG = -1e30
EXP2_SCALE = math.log2(math.e) / math.sqrt(HEAD)
PEERS = [
    (1, 0, 0), (0, 1, 0), (0, 3, 0), (1, 1, 0), (0, 2, 0), (1, 3, 0), (0, 1, 1), (1, 2, 0),
    (0, 3, 1), (1, 0, 1), (0, 2, 1), (1, 1, 1), (1, 3, 1), (1, 2, 1), (0, 0, 1),
]


def place(ds, dy, dc):
    dp = lax.axis_index("dp")
    ctx = lax.axis_index("ctx")
    side = dp % 2
    to_side = (side + ds) % 2
    to_ctx = ((ctx // 2 + dy) % 4) * 2 + (ctx % 2 + dc) % 2
    return (dp - side + to_side, to_ctx), to_side * 8 + to_ctx


def kernel(
    meta_ref, proj_ref, w_ref, out_ref,
    q_recv, k_recv, v_recv, meta_recv, meta_smem, k_pack, v_pack, probs, sent, merged, w_all, tiles,
    send_sem, recv_sem, meta_send, meta_sem, out_send, out_sem, w_sem, w_sends, local_sem,
):
    recv = (q_recv, k_recv, v_recv)
    me = (lax.axis_index("dp") % 2) * 8 + lax.axis_index("ctx")

    def columns(rank, kind):
        return pl.ds(pl.multiple_of(rank * (3 * HEAD) + kind * HEAD, HEAD), HEAD)

    dp = lax.axis_index("dp")
    ctx = lax.axis_index("ctx")
    x, z, core = dp // N_Z, dp % N_Z, ctx % 2
    shard, features = w_ref.shape
    half = pl.ds(pl.multiple_of(core * (features // 2), HEAD), features // 2)
    sibling = (dp, ctx - core + (core + 1) % 2)
    right = (x * N_Z + (z + 1) % N_Z, ctx)
    left = (x * N_Z + (z + N_Z - 1) % N_Z, ctx)
    across = [(((x + dx) % N_X) * N_Z + z, ctx) for dx in range(1, N_X)]

    own = []
    for kind in range(3):
        own.append(
            pltpu.make_async_copy(
                proj_ref.at[:, :, columns(me, kind)], recv[kind].at[pl.ds(2 * me, 2)], local_sem.at[kind]
            )
        )
    own.append(pltpu.make_async_copy(meta_ref, meta_recv.at[me], local_sem.at[3]))
    own.append(pltpu.make_async_copy(w_ref, w_all.at[dp], local_sem.at[5]))
    for copy in own:
        copy.start()

    barrier = pltpu.get_barrier_semaphore()
    greet = [place(*peer)[0] for peer in PEERS] + across
    greet.append((x * N_Z + (z + N_Z - 1 + 2 * (z % 2)) % N_Z, ctx))
    for device in greet:
        pl.semaphore_signal(barrier, inc=1, device_id=device, device_id_type=MESH)
    pl.semaphore_wait(barrier, len(greet))

    def chunk(dx, dz):
        return ((x + dx) % N_X) * N_Z + (z + N_Z + dz) % N_Z

    def weight_copy(at, device, sender, first=False, sem=None):
        return pltpu.make_async_remote_copy(
            src_ref=w_ref.at[:, half] if first else w_all.at[at, :, half], dst_ref=w_all.at[at, :, half],
            send_sem=w_sends.at[sender], recv_sem=w_sem.at[at] if sem is None else sem,
            device_id=device, device_id_type=MESH,
        )

    def hand_over(at):
        weight_copy(at, sibling, 0, sem=w_sem.at[N_X * N_Z]).start()

    def spread(at, first=False):
        for i in range(N_X - 1):
            weight_copy(at, across[i], 1 + i, first).start()
        if not first:
            hand_over(at)

    def ring_step(n):
        at = chunk(0, -n)
        weight_copy(at, right, N_X).wait_recv()
        if n < N_Z // 2:
            weight_copy(at, right, N_X).start()
        spread(at)
        if n < N_Z // 2:
            at = chunk(0, n)
            weight_copy(at, left, N_X + 1).wait_recv()
            if n < N_Z // 2 - 1:
                weight_copy(at, left, N_X + 1).start()
            spread(at)

    def drain(n):
        steps = [0] if n == 0 else [-n] if n == N_Z // 2 else [-n, n]
        for dz in steps:
            for i in range(N_X - 1):
                at = chunk(i + 1, dz)
                weight_copy(at, across[i], 1 + i).wait_recv()
                hand_over(at)

    started = []

    def issue(messages):
        for kind, i in messages:
            device, rank = place(*PEERS[i])
            started.append(
                pltpu.make_async_remote_copy(
                    src_ref=proj_ref.at[:, :, columns(rank, kind)], dst_ref=recv[kind].at[pl.ds(2 * me, 2)],
                    send_sem=send_sem.at[kind, i], recv_sem=recv_sem.at[kind, me],
                    device_id=device, device_id_type=MESH,
                )
            )
            started[-1].start()

    weight_copy(dp, right, N_X, True).start()
    weight_copy(dp, left, N_X + 1, True).start()
    for i, peer in enumerate(PEERS):
        device, rank = place(*peer)
        started.append(
            pltpu.make_async_remote_copy(
                src_ref=meta_ref, dst_ref=meta_recv.at[me], send_sem=meta_send.at[i],
                recv_sem=meta_sem.at[me], device_id=device, device_id_type=MESH,
            )
        )
        started[-1].start()
    messages = [(kind, i) for kind in (1, 0, 2) for i in range(len(PEERS))]
    issue(messages[:FIRST])
    spread(dp, True)
    for n in range(1, EARLY + 1):
        ring_step(n)
        if n >= 2:
            drain(n - 2)
        issue(messages[FIRST + (n - 1) * BATCH : FIRST + n * BATCH])
    issue(messages[FIRST + EARLY * BATCH :])

    def wait_kind(kind):
        for i, peer in enumerate(PEERS):
            device, rank = place(*peer)
            pltpu.make_async_remote_copy(
                src_ref=recv[kind].at[pl.ds(2 * rank, 2)], dst_ref=recv[kind].at[pl.ds(2 * rank, 2)],
                send_sem=send_sem.at[kind, i], recv_sem=recv_sem.at[kind, rank],
                device_id=device, device_id_type=MESH,
            ).wait_recv()
        own[kind].wait()

    for i, peer in enumerate(PEERS):
        device, rank = place(*peer)
        pltpu.make_async_remote_copy(
            src_ref=meta_recv.at[rank], dst_ref=meta_recv.at[rank], send_sem=meta_send.at[i],
            recv_sem=meta_sem.at[rank], device_id=device, device_id_type=MESH,
        ).wait_recv()
    own[3].wait()
    to_smem = pltpu.make_async_copy(meta_recv, meta_smem, local_sem.at[4])
    to_smem.start()
    to_smem.wait()

    def source(pack, block):
        return meta_smem[pack * 8 + block // 2, 0, block % 2]

    def clip(pack, block):
        return meta_smem[pack * 8, 0, 2 + block]

    def window(pack, block):
        first = block
        for back in range(1, WIN):
            at = jnp.maximum(block - back, 0)
            first = jnp.where(clip(pack, at) == clip(pack, block), jnp.minimum(first, at), first)
        return jnp.minimum(first, PACK - WIN)

    def gather(kind, target):
        def step(i, carry):
            target[i, :, pl.ds(0, HEAD)] = recv[kind][source(i // PACK, i % PACK)]
            return carry

        lax.fori_loop(0, 2 * PACK, step, 0)

    v_pack[:, :, HEAD:] = jnp.ones((2 * PACK, BLK, HEAD), jnp.bfloat16)
    wait_kind(1)
    gather(1, k_pack)
    wait_kind(0)

    def score_step(i, carry):
        pack, block = i // PACK, i % PACK
        start = window(pack, block)
        queries = q_recv[source(pack, block)]
        keys = k_pack[pl.ds(pack * PACK + start, WIN)].reshape(WIN * BLK, HEAD)
        scores = lax.dot_general(queries, keys, (((1,), (1,)), ((), ())), preferred_element_type=jnp.float32)
        parts = []
        for w in range(WIN):
            bias = jnp.where(clip(pack, start + w) == clip(pack, block), 0.0, NEG)
            parts.append(scores[:, w * BLK : (w + 1) * BLK] + bias)
        top = functools.reduce(jnp.maximum, parts)
        row_max = jnp.max(top, axis=1, keepdims=True)
        for w in range(WIN):
            probs[i, :, w * BLK : (w + 1) * BLK] = jnp.exp2((parts[w] - row_max) * EXP2_SCALE).astype(jnp.bfloat16)
        return carry

    jobs = [(n, n - 2) for n in range(EARLY + 1, N_Z // 2 + 1)]
    jobs += [(None, N_Z // 2 - 1), (None, N_Z // 2)]
    per = 2 * PACK // len(jobs)
    for i, (n, m) in enumerate(jobs):
        last = 2 * PACK if i == len(jobs) - 1 else (i + 1) * per
        lax.fori_loop(i * per, last, score_step, 0)
        if n is not None:
            ring_step(n)
        drain(m)
    wait_kind(2)
    gather(2, v_pack)

    def attend(rank):
        pack = rank // 8
        for slot in range(2):
            block = (rank % 8) * 2 + slot
            i = pack * PACK + block
            values = v_pack[pl.ds(pack * PACK + window(pack, block), WIN)].reshape(WIN * BLK, 2 * HEAD)
            total = jnp.dot(probs[i], values, preferred_element_type=jnp.float32)
            sent[rank, slot] = (total[:, :HEAD] / total[:, HEAD:]).astype(jnp.bfloat16)

    def my_columns(rank):
        return pl.ds(pl.multiple_of(rank * HEAD, HEAD), HEAD)

    def send_step(k, carry):
        ds, dy, dc = k % 2, (k // 2) % 4, k // 8
        device, rank = place(ds, dy, dc)
        attend(rank)
        pltpu.make_async_remote_copy(
            src_ref=sent.at[rank], dst_ref=merged.at[:, :, my_columns(me)], send_sem=out_send.at[k],
            recv_sem=out_sem.at[me], device_id=device, device_id_type=MESH,
        ).start()
        return carry

    lax.fori_loop(1, GROUP, send_step, 0)
    attend(me)
    keep = pltpu.make_async_copy(sent.at[me], merged.at[:, :, my_columns(me)], local_sem.at[3])
    keep.start()
    keep.wait()
    for k in range(1, GROUP):
        device, rank = place(k % 2, (k // 2) % 4, k // 8)
        copy = pltpu.make_async_remote_copy(
            src_ref=sent.at[rank], dst_ref=merged.at[:, :, my_columns(rank)], send_sem=out_send.at[k],
            recv_sem=out_sem.at[rank], device_id=device, device_id_type=MESH,
        )
        copy.wait_send()
        copy.wait_recv()
    for copy in started:
        copy.wait_send()
    own[4].wait()
    pieces = N_X * N_Z - 1

    def weight_bytes(count, sender, sem=None):
        part = w_all.at[pl.ds(0, count), :, half]
        return pltpu.make_async_remote_copy(
            src_ref=part, dst_ref=part, send_sem=w_sends.at[sender],
            recv_sem=w_sem.at[N_X * N_Z] if sem is None else sem, device_id=sibling, device_id_type=MESH,
        )

    weight_bytes(pieces, 0).wait_recv()

    def project(n, carry):
        at = pl.ds(pl.multiple_of(n * TILE, TILE), TILE)
        tiles[n] = jnp.dot(
            merged[...].reshape(2 * BLK, -1), w_all[:, :, at].reshape(-1, TILE), preferred_element_type=jnp.float32
        ).astype(jnp.bfloat16)
        pltpu.make_async_copy(tiles.at[n], out_ref.at[:, at], local_sem.at[6 + n]).start()
        return carry

    count = features // TILE
    lax.fori_loop(0, count, project, 0)
    for n in range(count):
        pltpu.make_async_copy(tiles.at[n], out_ref.at[:, pl.ds(n * TILE, TILE)], local_sem.at[6 + n]).wait()
    weight_bytes(pieces, 0).wait_send()
    for i in range(1, N_X):
        weight_bytes(N_Z, i).wait_send()
    weight_bytes(N_Z // 2, N_X).wait_send()
    weight_bytes(N_Z // 2 - 1, N_X + 1).wait_send()


def body(projections, block_source, clip_ids, out_weight):
    rows, width = projections.shape
    heads = width // (3 * HEAD)
    shard, features = out_weight.shape
    meta = jnp.concatenate([block_source.reshape(-1) % (2 * PACK), clip_ids.reshape(-1)])
    meta = jnp.pad(meta[None, :], ((0, 7), (0, 128 - meta.shape[0])))
    kinds = pltpu.SemaphoreType.DMA((3, GROUP))
    ranks = pltpu.SemaphoreType.DMA((GROUP,))
    return pl.pallas_call(
        kernel,
        out_shape=jax.ShapeDtypeStruct((rows, features), jnp.bfloat16),
        in_specs=[pl.BlockSpec(memory_space=pl.ANY)] + [pl.BlockSpec(memory_space=pltpu.HBM)] * 2,
        out_specs=pl.BlockSpec(memory_space=pl.ANY),
        scratch_shapes=[
            pltpu.VMEM((2 * PACK, BLK, HEAD), jnp.bfloat16),
            pltpu.VMEM((2 * PACK, BLK, HEAD), jnp.bfloat16),
            pltpu.VMEM((2 * PACK, BLK, HEAD), jnp.bfloat16),
            pltpu.VMEM((GROUP, 8, 128), jnp.int32),
            pltpu.SMEM((GROUP, 8, 128), jnp.int32),
            pltpu.VMEM((2 * PACK, BLK, HEAD), jnp.bfloat16),
            pltpu.VMEM((2 * PACK, BLK, 2 * HEAD), jnp.bfloat16),
            pltpu.VMEM((2 * PACK, BLK, WIN * BLK), jnp.bfloat16),
            pltpu.VMEM((GROUP, 2, BLK, HEAD), jnp.bfloat16),
            pltpu.VMEM((2, BLK, heads * HEAD), jnp.bfloat16),
            pltpu.VMEM((N_X * N_Z, shard, features), jnp.bfloat16),
            pltpu.VMEM((features // TILE, rows, TILE), jnp.bfloat16),
            kinds, kinds, ranks, ranks, ranks, ranks,
            pltpu.SemaphoreType.DMA((N_X * N_Z + 1,)),
            pltpu.SemaphoreType.DMA((N_X + 2,)),
            pltpu.SemaphoreType.DMA((6 + features // TILE,)),
        ],
        compiler_params=pltpu.CompilerParams(
            collective_id=0, has_side_effects=True, vmem_limit_bytes=63 * 2**20
        ),
        name="attend",
    )(meta, projections.reshape(2, BLK, width), out_weight)


def solution(mesh):
    return jax.shard_map(
        body,
        mesh=mesh,
        in_specs=(P(("dp", "ctx"), None), P("dp", "ctx", None), P("dp", None), P("dp", None)),
        out_specs=P(("dp", "ctx"), None),
        check_vma=False,
    )
```
